32 devices in a mesh: left: 8 (over y, x, core), right: 4 (over z).
Axes of the slice: x: 2, y: 2, z: 4, core: 2. Of those that a mesh axis runs over, the one named last changes fastest.
Arguments:
- amplitudes: bfloat16 [1024, 8192], P('left', 'right'), may hold values from -1 to 1
- row_sector: int32 [1024, 1], P('left'), may hold values from 0 to 7; in each aligned block of 128 rows (0 to 127, 128 to 255, ...) at most 32 rows name the same one
- sector_owner: int32 [8], replicated, may hold values from 0 to 7, each once
Outputs:
- owner_gram: float32 [8, 256, 256], P('left', 'right')
The draws below stay inside these ranges and needn't reach their ends.
Inputs may be any that keep to these rules, and one draw needn't show every extreme that they name: `row_sector`: in each aligned block of 128 rows no sector appears more than 32 times, and some sector appears exactly 32 times in some block. `sector_owner`: each owner index appears once.
All inputs are finite; a program needn't handle non-finite values.
Results may differ from the reference program's by a relative error of at most 0.0003.
Values may be sent and summed in bfloat16 or wider, within the bound.
No kernel may reach another device: no remote copies, remote signals or barrier semaphores. Data moves between devices by JAX's collectives and lax.ppermute only.
A program may use at most 64 MiB of HBM per device.

```python
import math
import jax
import jax.numpy as jnp
import numpy as np
from jax import lax

MOST = 32
ROWS_DEV = 128
SECTORS = 8
CAPS = 256
NL = 1024
NR = 8192
N_LEFT = 8


def draw_amplitudes(key, part):
    shared_count = 64
    key_left = jax.random.fold_in(key, 11)
    key_right = jax.random.fold_in(key, 12)
    key_noise = jax.random.fold_in(key, 13)
    loadings = jax.random.normal(key_left, (NL, shared_count), jnp.float32)
    patterns = jax.random.normal(key_right, (NR, shared_count), jnp.float32)
    order = jnp.arange(shared_count, dtype=jnp.float32)
    spectrum = jnp.exp(-order / 16.0)
    noise_level = 2.83
    noise = jax.random.normal(key_noise, (NL, NR), jnp.float32)
    shared = jnp.dot(loadings * spectrum[None, :], patterns.T, precision=lax.Precision.HIGHEST)
    weight_total = jnp.sum(spectrum * spectrum) + noise_level * noise_level
    total = (shared + noise_level * noise) / jnp.sqrt(NR * weight_total)
    return jnp.clip(total, -1.0, 1.0).astype(jnp.bfloat16)


def deal_out(rng, own, number, rows, amount, top, reach, skew):
    order = jax.random.permutation(rng, amount)
    heavy_load, ordinary = load_shares(amount, rows * top, reach, skew, True), load_shares(amount, rows * top, reach, skew, False)
    places = jnp.arange(amount)

    def named(sizes, offset_by):
        used = int((sizes > 0).sum())
        fixed = max(1, used // 4)
        passed = fixed + (places - fixed + offset_by * (used - fixed)) % max(1, amount - fixed)
        return jnp.zeros((amount,), jnp.int32).at[order[jnp.where(places < fixed, places, passed)]].set(jnp.asarray(sizes, jnp.int32))

    sizes = jnp.where(number % 4 == 0, named(heavy_load, number // 4), named(ordinary, number - number // 4 - 1))
    mixed = jax.random.permutation(jax.random.fold_in(own, 3), amount)
    giver, sink = mixed[0:amount // 2 * 2:2], mixed[1:amount // 2 * 2:2]
    room = jnp.minimum(sizes[giver] - 1, reach - sizes[sink]) // 2
    room = jnp.where((giver == order[0]) | (sink == order[0]) | (sizes[sink] == 0), 0, jnp.maximum(room, 0))
    passed = jax.random.randint(jax.random.fold_in(own, 4), (amount // 2,), 0, 1 << 20) % (room + 1)
    sizes = sizes.at[giver].add(-passed).at[sink].add(passed)
    items = jnp.searchsorted(jnp.cumsum(sizes), jnp.arange(rows * top), side="right").astype(jnp.int32)
    listing = items.reshape(top, rows).T
    listing = listing[jax.random.permutation(jax.random.fold_in(own, 1), rows)]
    offset_by = jax.random.randint(jax.random.fold_in(own, 2), (rows, 1), 0, top)
    return jnp.take_along_axis(listing, (jnp.arange(top)[None, :] + offset_by) % top, axis=1)


def load_shares(amount, total, most, lean, full):
    portions = [(1 << 20) // math.isqrt(grade ** lean) + 1 for grade in range(1, amount + 1)]
    largest = most if full else min(most, max(-(-total // amount), total * portions[0] // sum(portions)))
    least = 1 if total - largest >= amount - 1 else 0
    holding, surplus = [largest] + [least] * (amount - 1), total - largest - least * (amount - 1)
    while surplus > 0:
        free = [i for i in range(1, amount) if holding[i] < largest] or [i for i in range(1, amount) if holding[i] < most]
        mass, left = sum([portions[i] for i in free]), surplus
        for i in free:
            more = min(most - holding[i], max(1, left * portions[i] // mass), surplus)
            holding[i] = holding[i] + more
            surplus = surplus - more
    return np.array(holding)


def setup_inputs(seed: int = 0) -> dict:
    splits = jax.random.split(jax.random.key(seed), 4)
    amplitudes = draw_amplitudes(jax.random.fold_in(splits[3], 71), 0)
    row_sector_keys = jax.random.split(jax.random.fold_in(splits[1], 1), NL // ROWS_DEV)
    row_sector_turns = jax.random.permutation(jax.random.fold_in(splits[1], 3), NL // ROWS_DEV)
    row_sector = jax.vmap(lambda own, number: deal_out(jax.random.fold_in(splits[1], 2), own, number, ROWS_DEV, SECTORS, 1, MOST, 2))(row_sector_keys, row_sector_turns).reshape((NL, 1))
    sector_owner = jax.random.permutation(splits[2], SECTORS).astype(jnp.int32)
    return dict(amplitudes=amplitudes, row_sector=row_sector, sector_owner=sector_owner)


def reference(amplitudes, row_sector, sector_owner):
    count = amplitudes.shape[0]
    sector = row_sector[:, 0]
    blocks = sector.reshape(N_LEFT, ROWS_DEV)
    onehot = (blocks[:, :, None] == jnp.arange(SECTORS, dtype=jnp.int32)[None, None, :]).astype(jnp.int32)
    before = jnp.cumsum(onehot, axis=1) - onehot
    rank = jnp.sum(before * onehot, axis=2).reshape(count).astype(jnp.int32)
    positions = jnp.arange(count, dtype=jnp.int32)
    slot = (positions // ROWS_DEV) * MOST + rank
    owner_row = sector_owner[sector]
    table = jnp.full((SECTORS, CAPS), count, dtype=jnp.int32).at[owner_row, slot].set(positions)
    padded = jnp.concatenate([amplitudes, jnp.zeros((1, amplitudes.shape[1]), amplitudes.dtype)], axis=0)

    def single(indices):
        picked = padded[indices].astype(jnp.float32)
        return jnp.dot(picked, picked.T, precision=lax.Precision.HIGHEST, preferred_element_type=jnp.float32)

    return lax.map(single, table)
```

```python
import functools

import jax
import jax.numpy as jnp
from jax import lax
from jax.experimental import pallas as pl
from jax.experimental.pallas import tpu as pltpu
from jax.sharding import PartitionSpec as P

MOST = 32
MIB = 1 << 20


def pack_kernel(owners_count, amplitudes_ref, sector_ref, owner_ref, *outs):
    row_count = sector_ref.shape[1]
    me = lax.axis_index("left")
    sector = sector_ref[...]
    sub = lax.broadcasted_iota(jnp.int32, (owners_count, row_count), 0)
    onehot = sub == sector
    eye = lax.broadcasted_iota(jnp.int32, (owners_count, owners_count), 0) == lax.broadcasted_iota(
        jnp.int32, (owners_count, owners_count), 1
    )
    owner_column = jnp.sum(jnp.where(eye, owner_ref[...], 0), axis=1, keepdims=True)
    owner_row = jnp.sum(jnp.where(onehot, owner_column, 0), axis=0, keepdims=True)
    earlier = lax.broadcasted_iota(jnp.int32, (row_count, row_count), 0) < lax.broadcasted_iota(
        jnp.int32, (row_count, row_count), 1
    )
    before = jnp.dot(
        onehot.astype(jnp.bfloat16), earlier.astype(jnp.bfloat16), preferred_element_type=jnp.float32
    )
    rank = jnp.sum(jnp.where(onehot, before, 0.0), axis=0, keepdims=True).astype(jnp.int32)
    target = (owner_row ^ me) * MOST + rank
    for k in range(owners_count):
        place = lax.broadcasted_iota(jnp.int32, (MOST, row_count), 0) + k * MOST
        select = (place == target).astype(jnp.bfloat16)
        outs[k][...] = jnp.dot(
            select, amplitudes_ref[...], preferred_element_type=jnp.float32
        ).astype(jnp.bfloat16)


def gram_kernel(owners_count, chunk_count, *refs):
    blocks = refs[:owners_count]
    outs = refs[owners_count:owners_count + chunk_count]
    gathered, total = refs[owners_count + chunk_count:]
    me = lax.axis_index("left")
    here = lax.axis_index("right")
    for k in range(owners_count):
        start = pl.multiple_of((me ^ k) * MOST, MOST)
        gathered[pl.ds(start, MOST), :] = blocks[k][...]
    total[...] = lax.dot_general(
        gathered[...], gathered[...], (((1,), (1,)), ((), ())), preferred_element_type=jnp.float32
    )
    rows = total.shape[0] // chunk_count
    for k in range(chunk_count):
        start = pl.multiple_of((here ^ k) * rows, rows)
        outs[k][...] = total[pl.ds(start, rows), :]


def per_device(amplitudes, row_sector, sector_owner):
    owners_count = lax.axis_size("left")
    chunk_count = lax.axis_size("right")
    row_count, columns = amplitudes.shape
    slots = owners_count * MOST
    vmem = pl.BlockSpec(memory_space=pltpu.VMEM)
    blocks = pl.pallas_call(
        functools.partial(pack_kernel, owners_count),
        out_shape=[jax.ShapeDtypeStruct((MOST, columns), jnp.bfloat16)] * owners_count,
        in_specs=[vmem] * 3,
        out_specs=[vmem] * owners_count,
        compiler_params=pltpu.CompilerParams(vmem_limit_bytes=8 * MIB),
        name="pack",
    )(amplitudes, row_sector.reshape(1, row_count), sector_owner.reshape(1, owners_count))
    received = [blocks[0]] + [None] * (owners_count - 1)
    for k in reversed(range(1, owners_count)):
        received[k] = lax.ppermute(blocks[k], "left", [(i, i ^ k) for i in range(owners_count)])
    rows = slots // chunk_count
    chunks = pl.pallas_call(
        functools.partial(gram_kernel, owners_count, chunk_count),
        out_shape=[jax.ShapeDtypeStruct((rows, slots), jnp.float32)] * chunk_count,
        in_specs=[vmem] * owners_count,
        out_specs=[vmem] * chunk_count,
        scratch_shapes=[
            pltpu.VMEM((slots, columns), jnp.bfloat16),
            pltpu.VMEM((slots, slots), jnp.float32),
        ],
        compiler_params=pltpu.CompilerParams(vmem_limit_bytes=4 * MIB + 2 * slots * (2 * columns + 4 * slots)),
        name="gram",
    )(*received)
    result = chunks[0]
    for k in range(1, chunk_count):
        result = result + lax.ppermute(chunks[k], "right", [(i, i ^ k) for i in range(chunk_count)])
    return result[None]


def solution(mesh):
    in_specs = (P("left", "right"), P("left", None), P())
    out_specs = P("left", "right", None)
    return jax.shard_map(
        per_device, mesh=mesh, in_specs=in_specs, out_specs=out_specs, check_vma=False
    )
```

```python
import functools

import jax
import jax.numpy as jnp
from jax import lax
from jax.experimental import pallas as pl
from jax.experimental.pallas import tpu as pltpu
from jax.sharding import PartitionSpec as P

MOST = 32
MIB = 1 << 20


def exchange_order(count):
    far = sorted(range(2, count, 2), key=lambda k: (bin(k).count("1"), -k))
    odd = sorted(range(3, count, 2), key=lambda k: (bin(k).count("1"), -k))
    return far + odd + list(range(1, min(count, 2)))


def pack_kernel(owners_count, amplitudes_hbm, sector_hbm, owner_hbm, *refs):
    outs = refs[:owners_count]
    amplitudes_ref, sector_ref, owner_ref, sems = refs[owners_count:]
    row_count = sector_ref.shape[1]
    copies = [
        pltpu.make_async_copy(source, place, sems.at[i])
        for i, (source, place) in enumerate(
            [(sector_hbm, sector_ref), (owner_hbm, owner_ref), (amplitudes_hbm, amplitudes_ref)]
        )
    ]
    for copy in copies:
        copy.start()
    me = lax.axis_index("left")
    copies[0].wait()
    copies[1].wait()
    sector = sector_ref[...]
    onehot = lax.broadcasted_iota(jnp.int32, (owners_count, row_count), 0) == sector
    square = (owners_count, owners_count)
    eye = lax.broadcasted_iota(jnp.int32, square, 0) == lax.broadcasted_iota(jnp.int32, square, 1)
    owner_column = jnp.sum(jnp.where(eye, owner_ref[...], 0), axis=1, keepdims=True)
    owner_row = jnp.sum(jnp.where(onehot, owner_column, 0), axis=0, keepdims=True)
    square = (row_count, row_count)
    earlier = lax.broadcasted_iota(jnp.int32, square, 0) < lax.broadcasted_iota(jnp.int32, square, 1)
    before = jnp.dot(
        onehot.astype(jnp.bfloat16), earlier.astype(jnp.bfloat16), preferred_element_type=jnp.float32
    )
    rank = jnp.sum(jnp.where(onehot, before, 0.0), axis=0, keepdims=True).astype(jnp.int32)
    target = (owner_row ^ me) * MOST + rank
    place = lax.broadcasted_iota(jnp.int32, (owners_count * MOST, row_count), 0)
    select = (place == target).astype(jnp.bfloat16)
    copies[2].wait()
    packed = jnp.dot(select, amplitudes_ref[...], preferred_element_type=jnp.float32)
    for k in range(owners_count):
        outs[k][...] = packed[k * MOST:(k + 1) * MOST].astype(jnp.bfloat16)


def gram_kernel(order, chunk_count, *refs):
    blocks = refs[:len(order)]
    outs = refs[len(order):len(order) + chunk_count]
    gathered, total = refs[len(order) + chunk_count:]
    me = lax.axis_index("left")
    here = lax.axis_index("right")
    for k, block in zip(order, blocks):
        gathered[pl.ds(pl.multiple_of((me ^ k) * MOST, MOST), MOST), :] = block[...]
    total[...] = lax.dot_general(
        gathered[...], gathered[...], (((1,), (1,)), ((), ())), preferred_element_type=jnp.float32
    )
    rows = total.shape[0] // chunk_count
    for k in range(chunk_count):
        outs[k][...] = total[pl.ds(pl.multiple_of((here ^ k) * rows, rows), rows), :]


def per_device(amplitudes, row_sector, sector_owner):
    owners_count = lax.axis_size("left")
    chunk_count = lax.axis_size("right")
    row_count, columns = amplitudes.shape
    slots = owners_count * MOST
    vmem = pl.BlockSpec(memory_space=pltpu.VMEM)
    hbm = pl.BlockSpec(memory_space=pltpu.HBM)
    inputs = (amplitudes, row_sector.reshape(1, row_count), sector_owner.reshape(1, owners_count))
    blocks = pl.pallas_call(
        functools.partial(pack_kernel, owners_count),
        out_shape=[jax.ShapeDtypeStruct((MOST, columns), jnp.bfloat16)] * owners_count,
        in_specs=[hbm] * 3,
        out_specs=[vmem] * owners_count,
        scratch_shapes=[
            pltpu.VMEM((row_count, columns), jnp.bfloat16),
            pltpu.VMEM((1, row_count), jnp.int32),
            pltpu.VMEM((1, owners_count), jnp.int32),
            pltpu.SemaphoreType.DMA((3,)),
        ],
        compiler_params=pltpu.CompilerParams(
            vmem_limit_bytes=4 * MIB + 8 * row_count * columns + 8 * slots * row_count
        ),
        name="pack",
    )(*[pltpu.with_memory_space_constraint(x, pltpu.HBM) for x in inputs])
    order = exchange_order(owners_count)
    received = [blocks[0]] + [
        lax.ppermute(blocks[k], "left", [(i, i ^ k) for i in range(owners_count)]) for k in order
    ]
    rows = slots // chunk_count
    chunks = pl.pallas_call(
        functools.partial(gram_kernel, [0] + order, chunk_count),
        out_shape=[jax.ShapeDtypeStruct((rows, slots), jnp.float32)] * chunk_count,
        in_specs=[vmem] * owners_count,
        out_specs=[vmem] * chunk_count,
        scratch_shapes=[
            pltpu.VMEM((slots, columns), jnp.bfloat16),
            pltpu.VMEM((slots, slots), jnp.float32),
        ],
        compiler_params=pltpu.CompilerParams(
            vmem_limit_bytes=4 * MIB + 2 * slots * (2 * columns + 4 * slots)
        ),
        name="gram",
    )(*received)
    result = chunks[0]
    for k in reversed(range(1, chunk_count)):
        result = result + lax.ppermute(chunks[k], "right", [(i, i ^ k) for i in range(chunk_count)])
    return result[None]


def solution(mesh):
    in_specs = (P("left", "right"), P("left", None), P())
    out_specs = P("left", "right", None)
    return jax.shard_map(
        per_device, mesh=mesh, in_specs=in_specs, out_specs=out_specs, check_vma=False
    )
```

```python
import functools

import jax
import jax.numpy as jnp
from jax import lax
from jax.experimental import pallas as pl
from jax.experimental.pallas import tpu as pltpu
from jax.sharding import PartitionSpec as P

MOST = 32
MIB = 1 << 20


def exchange_order(count):
    far = sorted(range(2, count, 2), key=lambda k: (bin(k).count("1"), -k))
    odd = sorted(range(3, count, 2), key=lambda k: (bin(k).count("1"), -k))
    return far + odd + list(range(1, min(count, 2)))


def pack_kernel(owners_count, amplitudes_hbm, sector_hbm, owner_hbm, *refs):
    outs = refs[:owners_count]
    amplitudes_ref, sector_ref, owner_ref, sems = refs[owners_count:]
    row_count = sector_ref.shape[1]
    copies = [
        pltpu.make_async_copy(source, place, sems.at[i])
        for i, (source, place) in enumerate(
            [(sector_hbm, sector_ref), (owner_hbm, owner_ref), (amplitudes_hbm, amplitudes_ref)]
        )
    ]
    for copy in copies:
        copy.start()
    me = lax.axis_index("left")
    copies[0].wait()
    copies[1].wait()
    sector = sector_ref[...]
    onehot = lax.broadcasted_iota(jnp.int32, (owners_count, row_count), 0) == sector
    square = (owners_count, owners_count)
    eye = lax.broadcasted_iota(jnp.int32, square, 0) == lax.broadcasted_iota(jnp.int32, square, 1)
    owner_column = jnp.sum(jnp.where(eye, owner_ref[...], 0), axis=1, keepdims=True)
    owner_row = jnp.sum(jnp.where(onehot, owner_column, 0), axis=0, keepdims=True)
    square = (row_count, row_count)
    earlier = lax.broadcasted_iota(jnp.int32, square, 0) < lax.broadcasted_iota(jnp.int32, square, 1)
    before = jnp.dot(
        onehot.astype(jnp.bfloat16), earlier.astype(jnp.bfloat16), preferred_element_type=jnp.float32
    )
    rank = jnp.sum(jnp.where(onehot, before, 0.0), axis=0, keepdims=True).astype(jnp.int32)
    target = (owner_row ^ me) * MOST + rank
    place = lax.broadcasted_iota(jnp.int32, (owners_count * MOST, row_count), 0)
    select = (place == target).astype(jnp.bfloat16)
    copies[2].wait()
    packed = jnp.dot(select, amplitudes_ref[...], preferred_element_type=jnp.float32)
    for k in range(owners_count):
        outs[k][...] = packed[k * MOST:(k + 1) * MOST].astype(jnp.bfloat16)


def gram_kernel(order, chunk_count, *refs):
    blocks = refs[:len(order)]
    outs = refs[len(order):len(order) + chunk_count]
    gathered, total = refs[len(order) + chunk_count:]
    me = lax.axis_index("left")
    here = lax.axis_index("right")
    for k, block in zip(order, blocks):
        gathered[pl.ds(pl.multiple_of((me ^ k) * MOST, MOST), MOST), :] = block[...]
    total[...] = lax.dot_general(
        gathered[...], gathered[...], (((1,), (1,)), ((), ())), preferred_element_type=jnp.float32
    )
    rows = total.shape[0] // chunk_count
    for k in range(chunk_count):
        outs[k][...] = total[pl.ds(pl.multiple_of(lax.rem(here + k, chunk_count) * rows, rows), rows), :]


def per_device(amplitudes, row_sector, sector_owner):
    owners_count = lax.axis_size("left")
    chunk_count = lax.axis_size("right")
    row_count, columns = amplitudes.shape
    slots = owners_count * MOST
    vmem = pl.BlockSpec(memory_space=pltpu.VMEM)
    hbm = pl.BlockSpec(memory_space=pltpu.HBM)
    inputs = (amplitudes, row_sector.reshape(1, row_count), sector_owner.reshape(1, owners_count))
    blocks = pl.pallas_call(
        functools.partial(pack_kernel, owners_count),
        out_shape=[jax.ShapeDtypeStruct((MOST, columns), jnp.bfloat16)] * owners_count,
        in_specs=[hbm] * 3,
        out_specs=[vmem] * owners_count,
        scratch_shapes=[
            pltpu.VMEM((row_count, columns), jnp.bfloat16),
            pltpu.VMEM((1, row_count), jnp.int32),
            pltpu.VMEM((1, owners_count), jnp.int32),
            pltpu.SemaphoreType.DMA((3,)),
        ],
        compiler_params=pltpu.CompilerParams(
            vmem_limit_bytes=4 * MIB + 8 * row_count * columns + 8 * slots * row_count
        ),
        name="pack",
    )(*[pltpu.with_memory_space_constraint(x, pltpu.HBM) for x in inputs])
    order = exchange_order(owners_count)
    received = [blocks[0]] + [
        lax.ppermute(blocks[k], "left", [(i, i ^ k) for i in range(owners_count)]) for k in order
    ]
    rows = slots // chunk_count
    chunks = pl.pallas_call(
        functools.partial(gram_kernel, [0] + order, chunk_count),
        out_shape=[jax.ShapeDtypeStruct((rows, slots), jnp.float32)] * chunk_count,
        in_specs=[vmem] * owners_count,
        out_specs=[vmem] * chunk_count,
        scratch_shapes=[
            pltpu.VMEM((slots, columns), jnp.bfloat16),
            pltpu.VMEM((slots, slots), jnp.float32),
        ],
        compiler_params=pltpu.CompilerParams(
            vmem_limit_bytes=4 * MIB + 2 * slots * (2 * columns + 4 * slots)
        ),
        name="gram",
    )(*received)
    result = chunks[0]
    for k in range(1, chunk_count):
        pairs = [(i, (i + k) % chunk_count) for i in range(chunk_count)]
        result = result + lax.ppermute(chunks[k], "right", pairs)
    return result[None]


def solution(mesh):
    in_specs = (P("left", "right"), P("left", None), P())
    out_specs = P("left", "right", None)
    return jax.shard_map(
        per_device, mesh=mesh, in_specs=in_specs, out_specs=out_specs, check_vma=False
    )
```

```python
import functools

import jax
import jax.numpy as jnp
from jax import lax
from jax.experimental import pallas as pl
from jax.experimental.pallas import tpu as pltpu
from jax.sharding import PartitionSpec as P

MOST = 32
MIB = 1 << 20
STEPS = 32700.0
SIZE_STEPS = 30000.0
TINY = 1e-36
HEADER = 8


def exchange_order(count):
    far = sorted(range(2, count, 2), key=lambda k: (bin(k).count("1"), -k))
    odd = sorted(range(3, count, 2), key=lambda k: (bin(k).count("1"), -k))
    return far + odd + list(range(1, min(count, 2)))


def pack_kernel(owners_count, amplitudes_hbm, sector_hbm, owner_hbm, *refs):
    outs = refs[:owners_count]
    amplitudes_ref, sector_ref, owner_ref, sems = refs[owners_count:]
    row_count = sector_ref.shape[1]
    copies = [
        pltpu.make_async_copy(source, place, sems.at[i])
        for i, (source, place) in enumerate(
            [(sector_hbm, sector_ref), (owner_hbm, owner_ref), (amplitudes_hbm, amplitudes_ref)]
        )
    ]
    for copy in copies:
        copy.start()
    me = lax.axis_index("left")
    copies[0].wait()
    copies[1].wait()
    sector = sector_ref[...]
    onehot = lax.broadcasted_iota(jnp.int32, (owners_count, row_count), 0) == sector
    square = (owners_count, owners_count)
    eye = lax.broadcasted_iota(jnp.int32, square, 0) == lax.broadcasted_iota(jnp.int32, square, 1)
    owner_column = jnp.sum(jnp.where(eye, owner_ref[...], 0), axis=1, keepdims=True)
    owner_row = jnp.sum(jnp.where(onehot, owner_column, 0), axis=0, keepdims=True)
    square = (row_count, row_count)
    earlier = lax.broadcasted_iota(jnp.int32, square, 0) < lax.broadcasted_iota(jnp.int32, square, 1)
    before = jnp.dot(
        onehot.astype(jnp.bfloat16), earlier.astype(jnp.bfloat16), preferred_element_type=jnp.float32
    )
    rank = jnp.sum(jnp.where(onehot, before, 0.0), axis=0, keepdims=True).astype(jnp.int32)
    target = (owner_row ^ me) * MOST + rank
    place = lax.broadcasted_iota(jnp.int32, (owners_count * MOST, row_count), 0)
    select = (place == target).astype(jnp.bfloat16)
    copies[2].wait()
    packed = jnp.dot(select, amplitudes_ref[...], preferred_element_type=jnp.float32)
    for k in range(owners_count):
        outs[k][...] = packed[k * MOST:(k + 1) * MOST].astype(jnp.bfloat16)


def scale_of(power):
    return jnp.exp2(power) * (1.0 / SIZE_STEPS)


def size_units(diagonal, power):
    return jnp.ceil(jnp.sqrt(diagonal) / scale_of(power))


def code_chunk(chunk, row_units, column_units, power, out):
    rows, slots = chunk.shape
    unit = scale_of(power)
    row_inverse = jnp.where(row_units > 0.0, 1.0 / (row_units * unit), 0.0)
    column_inverse = jnp.where(column_units > 0.0, STEPS / (column_units * unit), 0.0)
    coded = jnp.floor(chunk * row_inverse * column_inverse + 0.5)
    out[:rows, :] = coded.astype(jnp.int32).astype(jnp.int16)
    shape = (out.shape[0] - rows, slots)
    first = lax.broadcasted_iota(jnp.int32, shape, 0) == 0
    header = jnp.where(first, jnp.broadcast_to(column_units, shape), jnp.broadcast_to(power, shape))
    out[rows:, :] = header.astype(jnp.int32).astype(jnp.int16)


def gram_kernel(order, chunk_count, coded, *refs):
    blocks = refs[:len(order)]
    outs = refs[len(order):len(order) + chunk_count]
    gathered, total = refs[len(order) + chunk_count:]
    me = lax.axis_index("left")
    here = lax.axis_index("right")
    for k, block in zip(order, blocks):
        gathered[pl.ds(pl.multiple_of((me ^ k) * MOST, MOST), MOST), :] = block[...]
    gram = lax.dot_general(
        gathered[...], gathered[...], (((1,), (1,)), ((), ())), preferred_element_type=jnp.float32
    )
    total[...] = gram
    slots = total.shape[0]
    rows = slots // chunk_count
    if coded:
        down = lax.broadcasted_iota(jnp.int32, (slots, slots), 0)
        across = lax.broadcasted_iota(jnp.int32, (slots, slots), 1)
        diagonal = jnp.sum(jnp.where(down == across, gram, 0.0), axis=0, keepdims=True)
        largest = jnp.maximum(jnp.max(diagonal, axis=1, keepdims=True), TINY)
        power = jnp.ceil(0.5 * jnp.log2(largest))
        column_units = size_units(diagonal, power)
    for k in range(chunk_count):
        start = pl.multiple_of(lax.rem(here + k, chunk_count) * rows, rows)
        chunk = total[pl.ds(start, rows), :]
        if coded and k:
            own = lax.broadcasted_iota(jnp.int32, (rows, slots), 0) + start == across[:rows]
            row_units = jnp.sum(jnp.where(own, column_units, 0.0), axis=1, keepdims=True)
            code_chunk(chunk, row_units, column_units, power, outs[k])
        else:
            outs[k][...] = chunk


def sum_kernel(own_ref, *refs):
    messages, out = refs[:-1], refs[-1]
    rows, slots = own_ref.shape
    start = lax.axis_index("right") * rows
    down = lax.broadcasted_iota(jnp.int32, (rows, slots), 0) + start
    own = down == lax.broadcasted_iota(jnp.int32, (rows, slots), 1)
    result = own_ref[...]
    for message in messages:
        header = message[rows:, :].astype(jnp.int32).astype(jnp.float32)
        unit = scale_of(header[1:2])
        column_units = header[:1]
        row_units = jnp.sum(jnp.where(own, column_units, 0.0), axis=1, keepdims=True)
        coded = message[:rows, :].astype(jnp.int32).astype(jnp.float32)
        result = result + coded * (row_units * unit) * (column_units * unit * (1.0 / STEPS))
    out[...] = result


def per_device(amplitudes, row_sector, sector_owner):
    owners_count = lax.axis_size("left")
    chunk_count = lax.axis_size("right")
    row_count, columns = amplitudes.shape
    slots = owners_count * MOST
    vmem = pl.BlockSpec(memory_space=pltpu.VMEM)
    hbm = pl.BlockSpec(memory_space=pltpu.HBM)
    inputs = (amplitudes, row_sector.reshape(1, row_count), sector_owner.reshape(1, owners_count))
    blocks = pl.pallas_call(
        functools.partial(pack_kernel, owners_count),
        out_shape=[jax.ShapeDtypeStruct((MOST, columns), jnp.bfloat16)] * owners_count,
        in_specs=[hbm] * 3,
        out_specs=[vmem] * owners_count,
        scratch_shapes=[
            pltpu.VMEM((row_count, columns), jnp.bfloat16),
            pltpu.VMEM((1, row_count), jnp.int32),
            pltpu.VMEM((1, owners_count), jnp.int32),
            pltpu.SemaphoreType.DMA((3,)),
        ],
        compiler_params=pltpu.CompilerParams(
            vmem_limit_bytes=4 * MIB + 8 * row_count * columns + 8 * slots * row_count
        ),
        name="pack",
    )(*[pltpu.with_memory_space_constraint(x, pltpu.HBM) for x in inputs])
    order = exchange_order(owners_count)
    received = [blocks[0]] + [
        lax.ppermute(blocks[k], "left", [(i, i ^ k) for i in range(owners_count)]) for k in order
    ]
    rows = slots // chunk_count
    coded = 0.5 / STEPS * slots ** 0.5 < 0.00025 and rows % 8 == 0
    whole = jax.ShapeDtypeStruct((rows, slots), jnp.float32)
    message = jax.ShapeDtypeStruct((rows + HEADER, slots), jnp.int16) if coded else whole
    chunks = pl.pallas_call(
        functools.partial(gram_kernel, [0] + order, chunk_count, coded),
        out_shape=[whole] + [message] * (chunk_count - 1),
        in_specs=[vmem] * owners_count,
        out_specs=[vmem] * chunk_count,
        scratch_shapes=[
            pltpu.VMEM((slots, columns), jnp.bfloat16),
            pltpu.VMEM((slots, slots), jnp.float32),
        ],
        compiler_params=pltpu.CompilerParams(
            vmem_limit_bytes=4 * MIB + 2 * slots * (2 * columns + 4 * slots)
        ),
        name="gram",
    )(*received)
    arrived = [chunks[0]]
    for k in range(1, chunk_count):
        pairs = [(i, (i + k) % chunk_count) for i in range(chunk_count)]
        arrived.append(lax.ppermute(chunks[k], "right", pairs))
    if not coded:
        return sum(arrived[1:], arrived[0])[None]
    result = pl.pallas_call(
        sum_kernel,
        out_shape=whole,
        in_specs=[vmem] * chunk_count,
        out_specs=vmem,
        compiler_params=pltpu.CompilerParams(vmem_limit_bytes=4 * MIB),
        name="sum",
    )(*arrived)
    return result[None]


def solution(mesh):
    in_specs = (P("left", "right"), P("left", None), P())
    out_specs = P("left", "right", None)
    return jax.shard_map(
        per_device, mesh=mesh, in_specs=in_specs, out_specs=out_specs, check_vma=False
    )
```

```python
import functools

import jax
import jax.numpy as jnp
from jax import lax
from jax.experimental import pallas as pl
from jax.experimental.pallas import tpu as pltpu
from jax.sharding import PartitionSpec as P

MOST = 32
MIB = 1 << 20
STEPS = 32700.0
SIZE_STEPS = 30000.0
TINY = 1e-36
HEADER = 8


def exchange_order(count):
    far = sorted(range(2, count, 2), key=lambda k: (bin(k).count("1"), -k))
    odd = sorted(range(3, count, 2), key=lambda k: (bin(k).count("1"), -k))
    return far + odd + list(range(1, min(count, 2)))


def pack_kernel(owners_count, amplitudes_hbm, sector_hbm, owner_hbm, *refs):
    outs = refs[:owners_count]
    amplitudes_ref, sector_ref, owner_ref, sems = refs[owners_count:]
    row_count = sector_ref.shape[1]
    copies = [
        pltpu.make_async_copy(source, place, sems.at[i])
        for i, (source, place) in enumerate(
            [(sector_hbm, sector_ref), (owner_hbm, owner_ref), (amplitudes_hbm, amplitudes_ref)]
        )
    ]
    for copy in copies:
        copy.start()
    me = lax.axis_index("left")
    copies[0].wait()
    copies[1].wait()
    sector = sector_ref[...]
    onehot = lax.broadcasted_iota(jnp.int32, (owners_count, row_count), 0) == sector
    square = (owners_count, owners_count)
    eye = lax.broadcasted_iota(jnp.int32, square, 0) == lax.broadcasted_iota(jnp.int32, square, 1)
    owner_column = jnp.sum(jnp.where(eye, owner_ref[...], 0), axis=1, keepdims=True)
    owner_row = jnp.sum(jnp.where(onehot, owner_column, 0), axis=0, keepdims=True)
    square = (row_count, row_count)
    earlier = lax.broadcasted_iota(jnp.int32, square, 0) < lax.broadcasted_iota(jnp.int32, square, 1)
    before = jnp.dot(
        onehot.astype(jnp.bfloat16), earlier.astype(jnp.bfloat16), preferred_element_type=jnp.float32
    )
    rank = jnp.sum(jnp.where(onehot, before, 0.0), axis=0, keepdims=True).astype(jnp.int32)
    target = (owner_row ^ me) * MOST + rank
    place = lax.broadcasted_iota(jnp.int32, (owners_count * MOST, row_count), 0)
    select = (place == target).astype(jnp.bfloat16)
    copies[2].wait()
    packed = jnp.dot(select, amplitudes_ref[...], preferred_element_type=jnp.float32)
    for k in range(owners_count):
        outs[k][...] = packed[k * MOST:(k + 1) * MOST].astype(jnp.bfloat16)


def scale_of(power):
    return jnp.exp2(power) * (1.0 / SIZE_STEPS)


def size_units(squares, power):
    return jnp.ceil(jnp.sqrt(squares) / scale_of(power))


def squares_at(block, source, slots):
    wide = block.astype(jnp.float32)
    column = jnp.sum(wide * wide, axis=1, keepdims=True)
    lane = lax.broadcasted_iota(jnp.int32, (MOST, slots), 1) - source * MOST
    here = lane == lax.broadcasted_iota(jnp.int32, (MOST, slots), 0)
    return jnp.sum(jnp.where(here, column, 0.0), axis=0, keepdims=True)


def place_kernel(order, coded, *refs):
    blocks, (gathered, squares) = refs[:len(order)], refs[len(order):]
    slots = gathered.shape[0]
    me = lax.axis_index("left")
    total = jnp.zeros((1, slots), jnp.float32)
    for k, block in zip(order, blocks):
        gathered[pl.ds(pl.multiple_of((me ^ k) * MOST, MOST), MOST), :] = block[...]
        if coded:
            total = total + squares_at(block[...], me ^ k, slots)
    squares[...] = total


def code_chunk(chunk, row_units, column_units, power, out):
    rows, slots = chunk.shape
    unit = scale_of(power)
    row_inverse = jnp.where(row_units > 0.0, 1.0 / (row_units * unit), 0.0)
    column_inverse = jnp.where(column_units > 0.0, STEPS / (column_units * unit), 0.0)
    coded = jnp.floor(chunk * row_inverse * column_inverse + 0.5)
    out[:rows, :] = coded.astype(jnp.int32).astype(jnp.int16)
    shape = (out.shape[0] - rows, slots)
    first = lax.broadcasted_iota(jnp.int32, shape, 0) == 0
    header = jnp.where(first, jnp.broadcast_to(column_units, shape), jnp.broadcast_to(power, shape))
    out[rows:, :] = header.astype(jnp.int32).astype(jnp.int16)


def gram_kernel(late, chunk_count, coded, placed, squares, *refs):
    blocks = refs[:len(late)]
    gathered, *outs = refs[len(late):]
    slots = gathered.shape[0]
    rows = slots // chunk_count
    me = lax.axis_index("left")
    here = lax.axis_index("right")
    for k, block in zip(late, blocks):
        gathered[pl.ds(pl.multiple_of((me ^ k) * MOST, MOST), MOST), :] = block[...]
    starts = [
        pl.multiple_of(lax.rem(here + k, chunk_count) * rows, rows) for k in range(chunk_count)
    ]
    if coded:
        diagonal = squares[...]
        for k, block in zip(late, blocks):
            diagonal = diagonal + squares_at(block[...], me ^ k, slots)
        largest = jnp.maximum(jnp.max(diagonal, axis=1, keepdims=True), TINY)
        power = jnp.ceil(0.5 * jnp.log2(largest))
        column_units = size_units(diagonal, power)
        down = lax.broadcasted_iota(jnp.int32, (rows, slots), 0)
        across = lax.broadcasted_iota(jnp.int32, (rows, slots), 1)
        row_units = [
            jnp.sum(jnp.where(down + start == across, column_units, 0.0), axis=1, keepdims=True)
            for start in starts
        ]
    turned = jnp.concatenate([gathered[pl.ds(start, rows), :] for start in starts], axis=0)
    total = lax.dot_general(
        turned, gathered[...], (((1,), (1,)), ((), ())), preferred_element_type=jnp.float32
    )
    for k in range(chunk_count):
        chunk = total[k * rows:(k + 1) * rows]
        if coded and k:
            code_chunk(chunk, row_units[k], column_units, power, outs[k])
        else:
            outs[k][...] = chunk


def sum_kernel(own_ref, *refs):
    messages, out = refs[:-1], refs[-1]
    rows, slots = own_ref.shape
    start = lax.axis_index("right") * rows
    down = lax.broadcasted_iota(jnp.int32, (rows, slots), 0) + start
    own = down == lax.broadcasted_iota(jnp.int32, (rows, slots), 1)
    result = own_ref[...]
    for message in messages:
        header = message[rows:, :].astype(jnp.int32).astype(jnp.float32)
        unit = scale_of(header[1:2])
        column_units = header[:1]
        row_units = jnp.sum(jnp.where(own, column_units, 0.0), axis=1, keepdims=True)
        coded = message[:rows, :].astype(jnp.int32).astype(jnp.float32)
        result = result + coded * (row_units * unit) * (column_units * unit * (1.0 / STEPS))
    out[...] = result


def per_device(amplitudes, row_sector, sector_owner):
    owners_count = lax.axis_size("left")
    chunk_count = lax.axis_size("right")
    row_count, columns = amplitudes.shape
    slots = owners_count * MOST
    vmem = pl.BlockSpec(memory_space=pltpu.VMEM)
    hbm = pl.BlockSpec(memory_space=pltpu.HBM)
    inputs = (amplitudes, row_sector.reshape(1, row_count), sector_owner.reshape(1, owners_count))
    blocks = pl.pallas_call(
        functools.partial(pack_kernel, owners_count),
        out_shape=[jax.ShapeDtypeStruct((MOST, columns), jnp.bfloat16)] * owners_count,
        in_specs=[hbm] * 3,
        out_specs=[vmem] * owners_count,
        scratch_shapes=[
            pltpu.VMEM((row_count, columns), jnp.bfloat16),
            pltpu.VMEM((1, row_count), jnp.int32),
            pltpu.VMEM((1, owners_count), jnp.int32),
            pltpu.SemaphoreType.DMA((3,)),
        ],
        compiler_params=pltpu.CompilerParams(
            vmem_limit_bytes=4 * MIB + 8 * row_count * columns + 8 * slots * row_count
        ),
        name="pack",
    )(*[pltpu.with_memory_space_constraint(x, pltpu.HBM) for x in inputs])
    order = exchange_order(owners_count)
    received = {0: blocks[0]}
    for k in order:
        received[k] = lax.ppermute(blocks[k], "left", [(i, i ^ k) for i in range(owners_count)])
    rows = slots // chunk_count
    coded = 0.5 / STEPS * slots ** 0.5 < 0.00025 and rows % 8 == 0
    whole = jax.ShapeDtypeStruct((rows, slots), jnp.float32)
    message = jax.ShapeDtypeStruct((rows + HEADER, slots), jnp.int16) if coded else whole
    late = order[-2:-1] or order
    early = [k for k in [0] + order if k not in late]
    placed, squares = pl.pallas_call(
        functools.partial(place_kernel, early, coded),
        out_shape=[
            jax.ShapeDtypeStruct((slots, columns), jnp.bfloat16),
            jax.ShapeDtypeStruct((1, slots), jnp.float32),
        ],
        in_specs=[vmem] * len(early),
        out_specs=[vmem] * 2,
        compiler_params=pltpu.CompilerParams(vmem_limit_bytes=4 * MIB + 2 * slots * columns),
        name="place",
    )(*[received[k] for k in early])
    gathered, *chunks = pl.pallas_call(
        functools.partial(gram_kernel, late, chunk_count, coded),
        out_shape=[jax.ShapeDtypeStruct((slots, columns), jnp.bfloat16), whole]
        + [message] * (chunk_count - 1),
        in_specs=[vmem] * (2 + len(late)),
        out_specs=[vmem] * (1 + chunk_count),
        input_output_aliases={0: 0},
        compiler_params=pltpu.CompilerParams(
            vmem_limit_bytes=4 * MIB + 2 * slots * (2 * columns + 4 * slots)
        ),
        name="gram",
    )(placed, squares, *[received[k] for k in late])
    arrived = [chunks[0]]
    for k in range(1, chunk_count):
        pairs = [(i, (i + k) % chunk_count) for i in range(chunk_count)]
        arrived.append(lax.ppermute(chunks[k], "right", pairs))
    if not coded:
        return sum(arrived[1:], arrived[0])[None]
    result = pl.pallas_call(
        sum_kernel,
        out_shape=whole,
        in_specs=[vmem] * chunk_count,
        out_specs=vmem,
        compiler_params=pltpu.CompilerParams(vmem_limit_bytes=4 * MIB),
        name="sum",
    )(*arrived)
    return result[None]


def solution(mesh):
    in_specs = (P("left", "right"), P("left", None), P())
    out_specs = P("left", "right", None)
    return jax.shard_map(
        per_device, mesh=mesh, in_specs=in_specs, out_specs=out_specs, check_vma=False
    )
```

```python
import functools

import jax
import jax.numpy as jnp
from jax import lax
from jax.experimental import pallas as pl
from jax.experimental.pallas import tpu as pltpu
from jax.sharding import PartitionSpec as P

MOST = 32
MIB = 1 << 20
STEPS = 32700.0
SIZE_STEPS = 30000.0
TINY = 1e-36
HEADER = 8


def exchange_steps(count):
    def ordered(first):
        return sorted(range(first, count, 2), key=lambda k: (bin(k).count("1"), -k))

    def mixed(partners, mask):
        plain, both, waiting = [], [], list(partners)
        while waiting:
            a = waiting.pop(0)
            even = bin(a & mask).count("1") % 2 == 0
            if even and waiting and bin(a).count("1") == bin(waiting[0]).count("1"):
                b = waiting.pop(0)
                both += [(a, b, mask), (b, a, mask)]
            else:
                plain.append((a, a, 0))
        return plain, both

    near = [(1, 1, 0)] if count > 1 else []
    even, even_both = mixed(ordered(2), 1)
    odd, odd_both = mixed(ordered(3), count - 1)
    return even + odd_both + even_both + odd + near


def partner_bits(me, step):
    a, b, mask = step
    bits = me & mask
    parity = 0
    while mask:
        parity, bits, mask = parity ^ (bits & 1), bits >> 1, mask >> 1
    return a + (b - a) * parity


def pack_kernel(owners_count, steps, amplitudes_hbm, sector_hbm, owner_hbm, *refs):
    outs = refs[:len(steps)]
    amplitudes_ref, sector_ref, owner_ref, sems = refs[len(steps):]
    row_count = sector_ref.shape[1]
    copies = [
        pltpu.make_async_copy(source, place, sems.at[i])
        for i, (source, place) in enumerate(
            [(sector_hbm, sector_ref), (owner_hbm, owner_ref), (amplitudes_hbm, amplitudes_ref)]
        )
    ]
    for copy in copies:
        copy.start()
    me = lax.axis_index("left")
    copies[0].wait()
    copies[1].wait()
    sector = sector_ref[...]
    onehot = lax.broadcasted_iota(jnp.int32, (owners_count, row_count), 0) == sector
    square = (owners_count, owners_count)
    eye = lax.broadcasted_iota(jnp.int32, square, 0) == lax.broadcasted_iota(jnp.int32, square, 1)
    owner_column = jnp.sum(jnp.where(eye, owner_ref[...], 0), axis=1, keepdims=True)
    owner_row = jnp.sum(jnp.where(onehot, owner_column, 0), axis=0, keepdims=True)
    square = (row_count, row_count)
    earlier = lax.broadcasted_iota(jnp.int32, square, 0) < lax.broadcasted_iota(jnp.int32, square, 1)
    before = jnp.dot(
        onehot.astype(jnp.bfloat16), earlier.astype(jnp.bfloat16), preferred_element_type=jnp.float32
    )
    rank = jnp.sum(jnp.where(onehot, before, 0.0), axis=0, keepdims=True).astype(jnp.int32)
    target = (owner_row ^ me) * MOST + rank
    place = lax.broadcasted_iota(jnp.int32, (MOST, row_count), 0)
    select = jnp.concatenate(
        [place + partner_bits(me, step) * MOST == target for step in steps], axis=0
    ).astype(jnp.bfloat16)
    copies[2].wait()
    packed = jnp.dot(select, amplitudes_ref[...], preferred_element_type=jnp.float32)
    for i, out in enumerate(outs):
        out[...] = packed[i * MOST:(i + 1) * MOST].astype(jnp.bfloat16)


def scale_of(power):
    return jnp.exp2(power) * (1.0 / SIZE_STEPS)


def size_units(squares, power):
    return jnp.ceil(jnp.sqrt(squares) / scale_of(power))


def squares_at(block, source, slots):
    wide = block.astype(jnp.float32)
    column = jnp.sum(wide * wide, axis=1, keepdims=True)
    lane = lax.broadcasted_iota(jnp.int32, (MOST, slots), 1) - source * MOST
    here = lane == lax.broadcasted_iota(jnp.int32, (MOST, slots), 0)
    return jnp.sum(jnp.where(here, column, 0.0), axis=0, keepdims=True)


def place_kernel(steps, coded, *refs):
    blocks, (gathered, squares) = refs[:len(steps)], refs[len(steps):]
    slots = gathered.shape[0]
    me = lax.axis_index("left")
    total = jnp.zeros((1, slots), jnp.float32)
    for step, block in zip(steps, blocks):
        source = me ^ partner_bits(me, step)
        gathered[pl.ds(pl.multiple_of(source * MOST, MOST), MOST), :] = block[...]
        if coded:
            total = total + squares_at(block[...], source, slots)
    squares[...] = total


def code_chunk(chunk, row_units, column_units, power, out):
    rows, slots = chunk.shape
    unit = scale_of(power)
    row_inverse = jnp.where(row_units > 0.0, 1.0 / (row_units * unit), 0.0)
    column_inverse = jnp.where(column_units > 0.0, STEPS / (column_units * unit), 0.0)
    coded = jnp.floor(chunk * row_inverse * column_inverse + 0.5)
    out[:rows, :] = coded.astype(jnp.int32).astype(jnp.int16)
    shape = (out.shape[0] - rows, slots)
    first = lax.broadcasted_iota(jnp.int32, shape, 0) == 0
    header = jnp.where(first, jnp.broadcast_to(column_units, shape), jnp.broadcast_to(power, shape))
    out[rows:, :] = header.astype(jnp.int32).astype(jnp.int16)


def gram_kernel(late, chunk_count, coded, placed, squares, *refs):
    blocks = refs[:len(late)]
    gathered, *outs = refs[len(late):]
    slots = gathered.shape[0]
    rows = slots // chunk_count
    me = lax.axis_index("left")
    here = lax.axis_index("right")
    sources = [me ^ partner_bits(me, step) for step in late]
    for source, block in zip(sources, blocks):
        gathered[pl.ds(pl.multiple_of(source * MOST, MOST), MOST), :] = block[...]
    starts = [
        pl.multiple_of(lax.rem(here + k, chunk_count) * rows, rows) for k in range(chunk_count)
    ]
    if coded:
        diagonal = squares[...]
        for source, block in zip(sources, blocks):
            diagonal = diagonal + squares_at(block[...], source, slots)
        largest = jnp.maximum(jnp.max(diagonal, axis=1, keepdims=True), TINY)
        power = jnp.ceil(0.5 * jnp.log2(largest))
        column_units = size_units(diagonal, power)
        down = lax.broadcasted_iota(jnp.int32, (rows, slots), 0)
        across = lax.broadcasted_iota(jnp.int32, (rows, slots), 1)
        row_units = [
            jnp.sum(jnp.where(down + start == across, column_units, 0.0), axis=1, keepdims=True)
            for start in starts
        ]
    turned = jnp.concatenate([gathered[pl.ds(start, rows), :] for start in starts], axis=0)
    total = lax.dot_general(
        turned, gathered[...], (((1,), (1,)), ((), ())), preferred_element_type=jnp.float32
    )
    for k in range(chunk_count):
        chunk = total[k * rows:(k + 1) * rows]
        if coded and k:
            code_chunk(chunk, row_units[k], column_units, power, outs[k])
        else:
            outs[k][...] = chunk


def sum_kernel(own_ref, *refs):
    messages, out = refs[:-1], refs[-1]
    rows, slots = own_ref.shape
    start = lax.axis_index("right") * rows
    down = lax.broadcasted_iota(jnp.int32, (rows, slots), 0) + start
    own = down == lax.broadcasted_iota(jnp.int32, (rows, slots), 1)
    result = own_ref[...]
    for message in messages:
        header = message[rows:, :].astype(jnp.int32).astype(jnp.float32)
        unit = scale_of(header[1:2])
        column_units = header[:1]
        row_units = jnp.sum(jnp.where(own, column_units, 0.0), axis=1, keepdims=True)
        coded = message[:rows, :].astype(jnp.int32).astype(jnp.float32)
        result = result + coded * (row_units * unit) * (column_units * unit * (1.0 / STEPS))
    out[...] = result


def per_device(amplitudes, row_sector, sector_owner):
    owners_count = lax.axis_size("left")
    chunk_count = lax.axis_size("right")
    row_count, columns = amplitudes.shape
    slots = owners_count * MOST
    vmem = pl.BlockSpec(memory_space=pltpu.VMEM)
    hbm = pl.BlockSpec(memory_space=pltpu.HBM)
    inputs = (amplitudes, row_sector.reshape(1, row_count), sector_owner.reshape(1, owners_count))
    steps = [(0, 0, 0)] + exchange_steps(owners_count)
    blocks = pl.pallas_call(
        functools.partial(pack_kernel, owners_count, steps),
        out_shape=[jax.ShapeDtypeStruct((MOST, columns), jnp.bfloat16)] * owners_count,
        in_specs=[hbm] * 3,
        out_specs=[vmem] * owners_count,
        scratch_shapes=[
            pltpu.VMEM((row_count, columns), jnp.bfloat16),
            pltpu.VMEM((1, row_count), jnp.int32),
            pltpu.VMEM((1, owners_count), jnp.int32),
            pltpu.SemaphoreType.DMA((3,)),
        ],
        compiler_params=pltpu.CompilerParams(
            vmem_limit_bytes=4 * MIB + 8 * row_count * columns + 8 * slots * row_count
        ),
        name="pack",
    )(*[pltpu.with_memory_space_constraint(x, pltpu.HBM) for x in inputs])
    received = {steps[0]: blocks[0]}
    for step, block in zip(steps[1:], blocks[1:]):
        pairs = [(i, i ^ partner_bits(i, step)) for i in range(owners_count)]
        received[step] = lax.ppermute(block, "left", pairs)
    rows = slots // chunk_count
    coded = 0.5 / STEPS * slots ** 0.5 < 0.00025 and rows % 8 == 0
    whole = jax.ShapeDtypeStruct((rows, slots), jnp.float32)
    message = jax.ShapeDtypeStruct((rows + HEADER, slots), jnp.int16) if coded else whole
    late = steps[1:][-2:-1] or steps[1:]
    early = [step for step in steps if step not in late]
    placed, squares = pl.pallas_call(
        functools.partial(place_kernel, early, coded),
        out_shape=[
            jax.ShapeDtypeStruct((slots, columns), jnp.bfloat16),
            jax.ShapeDtypeStruct((1, slots), jnp.float32),
        ],
        in_specs=[vmem] * len(early),
        out_specs=[vmem] * 2,
        compiler_params=pltpu.CompilerParams(vmem_limit_bytes=4 * MIB + 2 * slots * columns),
        name="place",
    )(*[received[step] for step in early])
    gathered, *chunks = pl.pallas_call(
        functools.partial(gram_kernel, late, chunk_count, coded),
        out_shape=[jax.ShapeDtypeStruct((slots, columns), jnp.bfloat16), whole]
        + [message] * (chunk_count - 1),
        in_specs=[vmem] * (2 + len(late)),
        out_specs=[vmem] * (1 + chunk_count),
        input_output_aliases={0: 0},
        compiler_params=pltpu.CompilerParams(
            vmem_limit_bytes=4 * MIB + 2 * slots * (2 * columns + 4 * slots)
        ),
        name="gram",
    )(placed, squares, *[received[step] for step in late])
    arrived = [chunks[0]]
    for k in range(1, chunk_count):
        pairs = [(i, (i + k) % chunk_count) for i in range(chunk_count)]
        arrived.append(lax.ppermute(chunks[k], "right", pairs))
    if not coded:
        return sum(arrived[1:], arrived[0])[None]
    result = pl.pallas_call(
        sum_kernel,
        out_shape=whole,
        in_specs=[vmem] * chunk_count,
        out_specs=vmem,
        compiler_params=pltpu.CompilerParams(vmem_limit_bytes=4 * MIB),
        name="sum",
    )(*arrived)
    return result[None]


def solution(mesh):
    in_specs = (P("left", "right"), P("left", None), P())
    out_specs = P("left", "right", None)
    return jax.shard_map(
        per_device, mesh=mesh, in_specs=in_specs, out_specs=out_specs, check_vma=False
    )
```

```python
import functools

import jax
import jax.numpy as jnp
from jax import lax
from jax.experimental import pallas as pl
from jax.experimental.pallas import tpu as pltpu
from jax.sharding import PartitionSpec as P

MOST = 32
MIB = 1 << 20
STEPS = 32700.0
SIZE_STEPS = 30000.0
TINY = 1e-36
HEADER = 8


def exchange_steps(count):
    def ordered(first):
        return sorted(range(first, count, 2), key=lambda k: (bin(k).count("1"), -k))

    def mixed(partners, mask):
        plain, both, waiting = [], [], list(partners)
        while waiting:
            a = waiting.pop(0)
            even = bin(a & mask).count("1") % 2 == 0
            if even and waiting and bin(a).count("1") == bin(waiting[0]).count("1"):
                b = waiting.pop(0)
                both += [(a, b, mask), (b, a, mask)]
            else:
                plain.append((a, a, 0))
        return plain, both

    near = [(1, 1, 0)] if count > 1 else []
    even, even_both = mixed(ordered(2), 1)
    odd, odd_both = mixed(ordered(3), count - 1)
    return even + odd_both + even_both[:1] + near + even_both[1:] + odd


def partner_bits(me, step):
    a, b, mask = step
    bits = me & mask
    parity = 0
    while mask:
        parity, bits, mask = parity ^ (bits & 1), bits >> 1, mask >> 1
    return a + (b - a) * parity


def pack_kernel(owners_count, steps, amplitudes_hbm, sector_hbm, owner_hbm, *refs):
    outs = refs[:len(steps)]
    amplitudes_ref, sector_ref, owner_ref, sems = refs[len(steps):]
    row_count = sector_ref.shape[1]
    copies = [
        pltpu.make_async_copy(source, place, sems.at[i])
        for i, (source, place) in enumerate(
            [(sector_hbm, sector_ref), (owner_hbm, owner_ref), (amplitudes_hbm, amplitudes_ref)]
        )
    ]
    for copy in copies:
        copy.start()
    me = lax.axis_index("left")
    copies[0].wait()
    copies[1].wait()
    sector = sector_ref[...]
    onehot = lax.broadcasted_iota(jnp.int32, (owners_count, row_count), 0) == sector
    square = (owners_count, owners_count)
    eye = lax.broadcasted_iota(jnp.int32, square, 0) == lax.broadcasted_iota(jnp.int32, square, 1)
    owner_column = jnp.sum(jnp.where(eye, owner_ref[...], 0), axis=1, keepdims=True)
    owner_row = jnp.sum(jnp.where(onehot, owner_column, 0), axis=0, keepdims=True)
    square = (row_count, row_count)
    earlier = lax.broadcasted_iota(jnp.int32, square, 0) < lax.broadcasted_iota(jnp.int32, square, 1)
    before = jnp.dot(
        onehot.astype(jnp.bfloat16), earlier.astype(jnp.bfloat16), preferred_element_type=jnp.float32
    )
    rank = jnp.sum(jnp.where(onehot, before, 0.0), axis=0, keepdims=True).astype(jnp.int32)
    target = (owner_row ^ me) * MOST + rank
    place = lax.broadcasted_iota(jnp.int32, (MOST, row_count), 0)
    select = jnp.concatenate(
        [place + partner_bits(me, step) * MOST == target for step in steps], axis=0
    ).astype(jnp.bfloat16)
    copies[2].wait()
    packed = jnp.dot(select, amplitudes_ref[...], preferred_element_type=jnp.float32)
    for i, out in enumerate(outs):
        out[...] = packed[i * MOST:(i + 1) * MOST].astype(jnp.bfloat16)


def scale_of(power):
    return jnp.exp2(power) * (1.0 / SIZE_STEPS)


def size_units(squares, power):
    return jnp.ceil(jnp.sqrt(squares) / scale_of(power))


def squares_at(block, source, slots):
    wide = block.astype(jnp.float32)
    column = jnp.sum(wide * wide, axis=1, keepdims=True)
    lane = lax.broadcasted_iota(jnp.int32, (MOST, slots), 1) - source * MOST
    here = lane == lax.broadcasted_iota(jnp.int32, (MOST, slots), 0)
    return jnp.sum(jnp.where(here, column, 0.0), axis=0, keepdims=True)


def place_kernel(steps, coded, *refs):
    blocks, (gathered, squares) = refs[:len(steps)], refs[len(steps):]
    slots = gathered.shape[0]
    me = lax.axis_index("left")
    total = jnp.zeros((1, slots), jnp.float32)
    for step, block in zip(steps, blocks):
        source = me ^ partner_bits(me, step)
        gathered[pl.ds(pl.multiple_of(source * MOST, MOST), MOST), :] = block[...]
        if coded:
            total = total + squares_at(block[...], source, slots)
    squares[...] = total


def code_chunk(chunk, row_units, column_units, power, out):
    rows, slots = chunk.shape
    unit = scale_of(power)
    row_inverse = jnp.where(row_units > 0.0, 1.0 / (row_units * unit), 0.0)
    column_inverse = jnp.where(column_units > 0.0, STEPS / (column_units * unit), 0.0)
    coded = jnp.floor(chunk * row_inverse * column_inverse + 0.5)
    out[:rows, :] = coded.astype(jnp.int32).astype(jnp.int16)
    shape = (out.shape[0] - rows, slots)
    first = lax.broadcasted_iota(jnp.int32, shape, 0) == 0
    header = jnp.where(first, jnp.broadcast_to(column_units, shape), jnp.broadcast_to(power, shape))
    out[rows:, :] = header.astype(jnp.int32).astype(jnp.int16)


def gram_kernel(late, chunk_count, coded, placed, squares, *refs):
    blocks = refs[:len(late)]
    gathered, *outs = refs[len(late):]
    slots = gathered.shape[0]
    rows = slots // chunk_count
    me = lax.axis_index("left")
    here = lax.axis_index("right")
    sources = [me ^ partner_bits(me, step) for step in late]
    for source, block in zip(sources, blocks):
        gathered[pl.ds(pl.multiple_of(source * MOST, MOST), MOST), :] = block[...]
    starts = [
        pl.multiple_of(lax.rem(here + k, chunk_count) * rows, rows) for k in range(chunk_count)
    ]
    if coded:
        diagonal = squares[...]
        for source, block in zip(sources, blocks):
            diagonal = diagonal + squares_at(block[...], source, slots)
        largest = jnp.maximum(jnp.max(diagonal, axis=1, keepdims=True), TINY)
        power = jnp.ceil(0.5 * jnp.log2(largest))
        column_units = size_units(diagonal, power)
        down = lax.broadcasted_iota(jnp.int32, (rows, slots), 0)
        across = lax.broadcasted_iota(jnp.int32, (rows, slots), 1)
        row_units = [
            jnp.sum(jnp.where(down + start == across, column_units, 0.0), axis=1, keepdims=True)
            for start in starts
        ]
    turned = jnp.concatenate([gathered[pl.ds(start, rows), :] for start in starts], axis=0)
    total = lax.dot_general(
        turned, gathered[...], (((1,), (1,)), ((), ())), preferred_element_type=jnp.float32
    )
    for k in range(chunk_count):
        chunk = total[k * rows:(k + 1) * rows]
        if coded and k:
            code_chunk(chunk, row_units[k], column_units, power, outs[k])
        else:
            outs[k][...] = chunk


def sum_kernel(own_ref, *refs):
    messages, out = refs[:-1], refs[-1]
    rows, slots = own_ref.shape
    start = lax.axis_index("right") * rows
    down = lax.broadcasted_iota(jnp.int32, (rows, slots), 0) + start
    own = down == lax.broadcasted_iota(jnp.int32, (rows, slots), 1)
    result = own_ref[...]
    for message in messages:
        header = message[rows:, :].astype(jnp.int32).astype(jnp.float32)
        unit = scale_of(header[1:2])
        column_units = header[:1]
        row_units = jnp.sum(jnp.where(own, column_units, 0.0), axis=1, keepdims=True)
        coded = message[:rows, :].astype(jnp.int32).astype(jnp.float32)
        result = result + coded * (row_units * unit) * (column_units * unit * (1.0 / STEPS))
    out[...] = result


def per_device(amplitudes, row_sector, sector_owner):
    owners_count = lax.axis_size("left")
    chunk_count = lax.axis_size("right")
    row_count, columns = amplitudes.shape
    slots = owners_count * MOST
    vmem = pl.BlockSpec(memory_space=pltpu.VMEM)
    hbm = pl.BlockSpec(memory_space=pltpu.HBM)
    inputs = (amplitudes, row_sector.reshape(1, row_count), sector_owner.reshape(1, owners_count))
    steps = [(0, 0, 0)] + exchange_steps(owners_count)
    blocks = pl.pallas_call(
        functools.partial(pack_kernel, owners_count, steps),
        out_shape=[jax.ShapeDtypeStruct((MOST, columns), jnp.bfloat16)] * owners_count,
        in_specs=[hbm] * 3,
        out_specs=[vmem] * owners_count,
        scratch_shapes=[
            pltpu.VMEM((row_count, columns), jnp.bfloat16),
            pltpu.VMEM((1, row_count), jnp.int32),
            pltpu.VMEM((1, owners_count), jnp.int32),
            pltpu.SemaphoreType.DMA((3,)),
        ],
        compiler_params=pltpu.CompilerParams(
            vmem_limit_bytes=4 * MIB + 8 * row_count * columns + 8 * slots * row_count
        ),
        name="pack",
    )(*[pltpu.with_memory_space_constraint(x, pltpu.HBM) for x in inputs])
    received = {steps[0]: blocks[0]}
    for step, block in zip(steps[1:], blocks[1:]):
        pairs = [(i, i ^ partner_bits(i, step)) for i in range(owners_count)]
        received[step] = lax.ppermute(block, "left", pairs)
    rows = slots // chunk_count
    coded = 0.5 / STEPS * slots ** 0.5 < 0.00025 and rows % 8 == 0
    whole = jax.ShapeDtypeStruct((rows, slots), jnp.float32)
    message = jax.ShapeDtypeStruct((rows + HEADER, slots), jnp.int16) if coded else whole
    late = steps[1:][-1:]
    early = [step for step in steps if step not in late]
    placed, squares = pl.pallas_call(
        functools.partial(place_kernel, early, coded),
        out_shape=[
            jax.ShapeDtypeStruct((slots, columns), jnp.bfloat16),
            jax.ShapeDtypeStruct((1, slots), jnp.float32),
        ],
        in_specs=[vmem] * len(early),
        out_specs=[vmem] * 2,
        compiler_params=pltpu.CompilerParams(vmem_limit_bytes=4 * MIB + 2 * slots * columns),
        name="place",
    )(*[received[step] for step in early])
    gathered, *chunks = pl.pallas_call(
        functools.partial(gram_kernel, late, chunk_count, coded),
        out_shape=[jax.ShapeDtypeStruct((slots, columns), jnp.bfloat16), whole]
        + [message] * (chunk_count - 1),
        in_specs=[vmem] * (2 + len(late)),
        out_specs=[vmem] * (1 + chunk_count),
        input_output_aliases={0: 0},
        compiler_params=pltpu.CompilerParams(
            vmem_limit_bytes=4 * MIB + 2 * slots * (2 * columns + 4 * slots)
        ),
        name="gram",
    )(placed, squares, *[received[step] for step in late])
    arrived = [chunks[0]]
    for k in range(1, chunk_count):
        pairs = [(i, (i + k) % chunk_count) for i in range(chunk_count)]
        arrived.append(lax.ppermute(chunks[k], "right", pairs))
    if not coded:
        return sum(arrived[1:], arrived[0])[None]
    result = pl.pallas_call(
        sum_kernel,
        out_shape=whole,
        in_specs=[vmem] * chunk_count,
        out_specs=vmem,
        compiler_params=pltpu.CompilerParams(vmem_limit_bytes=4 * MIB),
        name="sum",
    )(*arrived)
    return result[None]


def solution(mesh):
    in_specs = (P("left", "right"), P("left", None), P())
    out_specs = P("left", "right", None)
    return jax.shard_map(
        per_device, mesh=mesh, in_specs=in_specs, out_specs=out_specs, check_vma=False
    )
```
